32 devices in a mesh: alpha: 16 (over z, y, x), beta: 2 (over core).
Axes of the slice: x: 2, y: 2, z: 4, core: 2. Of those that a mesh axis runs over, the one named last changes fastest.
Arguments:
- coeffs: bfloat16 [1, 2048, 4096], P(None, 'alpha', 'beta'), may hold values from -6 to 6
- beta_list: int32 [32, 8], P('beta'), may hold values from 0 to 31
- beta_kind: int32 [32, 8], P('beta'), may hold values from 0 to 7
- opp_beta_kind: int32 [32, 8], P('beta'), may hold values from 0 to 7
- alpha_list: int32 [16, 4], replicated, may hold values from 0 to 15, as said below
- alpha_kind: int32 [16, 4], replicated, may hold values from 0 to 7
- opp_list: int32 [16, 3], replicated, may hold values from 0 to 15, as said below
- opp_kind: int32 [16, 3], replicated, may hold values from 0 to 7
- beta_table: bfloat16 [8, 128, 128], replicated, may hold values from -0.1875 to 0.1875
- alpha_table: bfloat16 [8, 128, 128], replicated, may hold values from -0.25 to 0.25
- opp_alpha_table: bfloat16 [8, 128, 128], replicated, may hold values from -0.3125 to 0.3125
- opp_beta_table: bfloat16 [8, 128, 128], replicated, may hold values from -0.1875 to 0.1875
Outputs:
- sigma_out: bfloat16 [1, 2048, 4096], P(None, 'alpha', 'beta')
The draws below stay inside these ranges and needn't reach their ends.
Inputs may be any that keep to these rules, and one draw needn't show every extreme that they name: `alpha_list`: each entry of row i lies within 3 of i; the entries of a row are distinct. `opp_list`: each entry of row i lies within 3 of i; the entries of a row are distinct.
All inputs are finite; a program needn't handle non-finite values.
Results may differ from the reference program's by a relative error of at most 0.0034.
Values may be sent and summed in bfloat16 or wider, within the bound.
A program may use at most 128 MiB of HBM per device.

```python
import jax
import jax.numpy as jnp
from jax import lax

TILE = 128
NB = 4096
ROOTS = 1
BETA_LINKS = 8
ALPHA_LINKS = 4
OPP_LINKS = 3
KINDS = 8
REACH = 3
NA = 2048


def pick_nearby(key, count):
    block_count = NA // TILE
    span_count = 2 * REACH + 1
    offsets = jnp.arange(span_count, dtype=jnp.int32) - REACH
    row_ids = jnp.arange(block_count, dtype=jnp.int32)[:, None]
    target = row_ids + offsets[None, :]
    inside = (target >= 0) & (target < block_count)
    scores = jax.random.randint(key, (block_count, span_count), 0, 1 << 20, dtype=jnp.int32) * span_count + jnp.arange(span_count, dtype=jnp.int32)[None, :]
    scores = jnp.where(inside, scores + 1, 0)
    unused, chosen = lax.top_k(scores, count)
    return jnp.take_along_axis(target, chosen, axis=1).astype(jnp.int32)


def draw_alpha_list(key, part):
    return pick_nearby(jax.random.fold_in(key, 11), ALPHA_LINKS)


def draw_opp_list(key, part):
    return pick_nearby(jax.random.fold_in(key, 23), OPP_LINKS)


def set_ends(array, own_key, smallest, high):
    longest = array.shape.index(max(array.shape))
    spots = []
    for shift in (0, 1):
        where = [jax.random.randint(jax.random.fold_in(own_key, axis), (), 0, length) for axis, length in enumerate(array.shape)]
        where[longest] = (where[longest] + shift) % array.shape[longest]
        spots.append(tuple(where))
    return array.at[spots[0]].set(smallest).at[spots[1]].set(high)


def block_scale(own_key, shape, pieces, least, top_value):
    def one(dim, parts):
        heights = jax.random.uniform(jax.random.fold_in(jax.random.fold_in(own_key, 6), dim), (parts,), jnp.float32, least / len(pieces), top_value / len(pieces))
        return jnp.repeat(jnp.exp(heights), shape[dim] // parts).reshape((-1,) + (1,) * (len(shape) - dim - 1))

    level = one(*pieces[0])
    for cut in pieces[1:]:
        level = level * one(*cut)
    return level


def normal_values(own_key, extent, spread, limit, split=(), kind=jnp.bfloat16):
    drawn = jax.random.normal(own_key, extent, jnp.float32) * spread
    if len(split) > 0:
        drawn = block_scale(own_key, extent, split, -0.22, 0.18) * drawn
    return jnp.clip(drawn, min=-limit, max=limit).astype(kind)


def setup_inputs(seed: int = 0) -> dict:
    keys = jax.random.split(jax.random.key(seed), 13)
    return {
        "coeffs": normal_values(keys[0], (ROOTS, NA, NB), 1.0, 6.0, ((1, 16), (2, 2))),
        "beta_list": set_ends(jax.random.randint(keys[1], (NB // TILE, BETA_LINKS), 0, NB // TILE), jax.random.fold_in(keys[1], 1), 0, (NB // TILE) - 1).astype(jnp.int32),
        "beta_kind": set_ends(jax.random.randint(keys[2], (NB // TILE, BETA_LINKS), 0, KINDS), jax.random.fold_in(keys[2], 1), 0, KINDS - 1).astype(jnp.int32),
        "opp_beta_kind": set_ends(jax.random.randint(keys[3], (NB // TILE, BETA_LINKS), 0, KINDS), jax.random.fold_in(keys[3], 1), 0, KINDS - 1).astype(jnp.int32),
        "alpha_list": draw_alpha_list(jax.random.fold_in(keys[12], 71), 0),
        "alpha_kind": set_ends(jax.random.randint(keys[5], (NA // TILE, ALPHA_LINKS), 0, KINDS), jax.random.fold_in(keys[5], 1), 0, KINDS - 1).astype(jnp.int32),
        "opp_list": draw_opp_list(jax.random.fold_in(keys[12], 71), 0),
        "opp_kind": set_ends(jax.random.randint(keys[7], (NA // TILE, OPP_LINKS), 0, KINDS), jax.random.fold_in(keys[7], 1), 0, KINDS - 1).astype(jnp.int32),
        "beta_table": normal_values(keys[8], (KINDS, TILE, TILE), (TILE * BETA_LINKS) ** -0.5, 0.1875),
        "alpha_table": normal_values(keys[9], (KINDS, TILE, TILE), (TILE * ALPHA_LINKS) ** -0.5, 0.25),
        "opp_alpha_table": normal_values(keys[10], (KINDS, TILE, TILE), (TILE * OPP_LINKS) ** -0.5, 0.3125),
        "opp_beta_table": normal_values(keys[11], (KINDS, TILE, TILE), (TILE * BETA_LINKS) ** -0.5, 0.1875),
    }


def beta_apply(row_data, sources, kind_ids, tile_table):
    root_count, row_count, col_count = row_data.shape
    tile_size = tile_table.shape[1]
    tiled = row_data.reshape(root_count, row_count, col_count // tile_size, tile_size)
    summed = jnp.zeros((root_count, row_count, sources.shape[0], tile_size), jnp.float32)
    for link in range(sources.shape[1]):
        picked = jnp.take(tiled, sources[:, link], axis=2).astype(jnp.float32)
        tile_sets = jnp.take(tile_table, kind_ids[:, link], axis=0).astype(jnp.float32)
        summed = summed + jnp.einsum("rajt,jst->rajs", picked, tile_sets, precision=lax.Precision.HIGHEST)
    return summed.reshape(root_count, row_count, -1)


def alpha_sum(blocks, sources, kind_ids, tile_table):
    summed = jnp.zeros((blocks.shape[0], blocks.shape[2], blocks.shape[3]), jnp.float32)
    for link in range(sources.shape[0]):
        picked = lax.dynamic_index_in_dim(blocks, sources[link], 1, keepdims=False).astype(jnp.float32)
        tile_one = lax.dynamic_index_in_dim(tile_table, kind_ids[link], 0, keepdims=False).astype(jnp.float32)
        summed = summed + jnp.einsum("st,rtc->rsc", tile_one, picked, precision=lax.Precision.HIGHEST)
    return summed


def reference(coeffs, beta_list, beta_kind, opp_beta_kind, alpha_list, alpha_kind, opp_list, opp_kind, beta_table, alpha_table, opp_alpha_table, opp_beta_table):
    root_count, alpha_count, beta_count = coeffs.shape
    tile_size = alpha_table.shape[1]
    block_count = alpha_count // tile_size
    blocks = coeffs.reshape(root_count, block_count, tile_size, beta_count)

    def one_block(block):
        own_rows = lax.dynamic_index_in_dim(blocks, block, 1, keepdims=False)
        beta_part = beta_apply(own_rows, beta_list, beta_kind, beta_table)
        alpha_part = alpha_sum(blocks, alpha_list[block], alpha_kind[block], alpha_table)
        half_sum = alpha_sum(blocks, opp_list[block], opp_kind[block], opp_alpha_table).astype(jnp.bfloat16)
        mixed_part = beta_apply(half_sum, beta_list, opp_beta_kind, opp_beta_table)
        return (beta_part + alpha_part + mixed_part).astype(jnp.bfloat16)

    result = lax.map(one_block, jnp.arange(block_count, dtype=jnp.int32))
    return jnp.transpose(result, (1, 0, 2, 3)).reshape(root_count, alpha_count, beta_count)
```

```python
import functools

import jax
import jax.numpy as jnp
from jax import lax
from jax.experimental import pallas as pl
from jax.experimental.pallas import tpu as pltpu
from jax.sharding import PartitionSpec as P

CHUNKS = 4
GROUP = 4
BF16, F32 = jnp.bfloat16, jnp.float32
LOW, HIGH, DIAG = range(3)


def picked_tile(block, lists, kinds, table, source):
    kind, found = jnp.int32(0), jnp.int32(0)
    for link in range(lists.shape[1]):
        hit = (lists[block, link] == source).astype(jnp.int32)
        kind += hit * kinds[block, link]
        found += hit
    return table[kind].astype(F32) * found.astype(F32)


def kernel(
    group_count,
    beta_list,
    beta_kind,
    opp_beta_kind,
    alpha_list,
    alpha_kind,
    opp_list,
    opp_kind,
    coeffs,
    beta_table,
    alpha_table,
    opp_alpha_table,
    opp_beta_table,
    out,
    plane,
    cross,
    whole,
    half,
    acc,
    tiles,
    own_send,
    plane_recv,
    relay_send,
    z_send,
    cross_recv,
    hop_send,
    pair_sem,
    half_send,
    half_recv,
):
    rows, cols = coeffs.shape
    width = cols // CHUNKS
    tile = beta_table.shape[1]
    per_half = cols // tile
    per_chunk = width // tile
    me, core = lax.axis_index("alpha"), lax.axis_index("beta")
    z, p = me // GROUP, me % GROUP
    x, y = p % 2, p // 2
    places = (p + 1 - 2 * x, p + 2 - 4 * y, 3 - p)
    mates = tuple(z * GROUP + q for q in places)
    steps = (1 - 2 * x, 1 - 2 * y, 1 - 2 * y)
    middle = x + y == 1

    def inside(group):
        return (group >= 0) & (group < group_count)

    has_out = [inside(z + step) for step in steps]
    has_in = [inside(z - step) for step in steps]

    def chip(index):
        return (index, core)

    pair = (me, 1 - core)

    def send(src, dst, send_sem, recv_sem, device):
        return pltpu.make_async_remote_copy(
            src_ref=src,
            dst_ref=dst,
            send_sem=send_sem,
            recv_sem=recv_sem,
            device_id=device,
            device_id_type=pl.DeviceIdType.MESH,
        )

    def columns(c):
        return pl.ds(c * width, width)

    def own_copy(to, c):
        return send(
            coeffs.at[:, columns(c)], plane.at[to, c], own_send.at[to, c], plane_recv.at[to, c], chip(mates[to])
        )

    def relay_copy(c):
        src, to = (LOW, HIGH) if c % 2 == 0 else (HIGH, LOW)
        return send(plane.at[src, c], plane.at[DIAG, c], relay_send.at[c], plane_recv.at[DIAG, c], chip(mates[to]))

    def z_copy(r, c):
        return send(
            plane.at[r, c], cross.at[r, c], z_send.at[r, c], cross_recv.at[r, c], chip(me + GROUP * steps[r])
        )

    def hop_copy(src, c):
        to = HIGH if src == LOW else LOW
        return send(cross.at[src, c], cross.at[DIAG, c], hop_send.at[src, c], cross_recv.at[DIAG, c], chip(mates[to]))

    def half_copy(c):
        part = half.at[pl.ds(core * per_half + c * per_chunk, per_chunk)]
        return send(part, part, half_send.at[c], half_recv.at[c], pair)

    def pair_copy(t):
        part = coeffs.at[:, pl.ds(t * tile, tile)]
        return send(part, whole.at[core * per_half + t], pair_sem.at[0, t], pair_sem.at[1, t], pair)

    barrier = pltpu.get_barrier_semaphore()
    for device in (chip(mates[LOW]), chip(mates[HIGH]), pair):
        pl.semaphore_signal(barrier, inc=1, device_id=device, device_id_type=pl.DeviceIdType.MESH)
    up, down = inside(z + 1), inside(z - 1)
    for there, offset in ((up, GROUP), (down, -GROUP)):

        @pl.when(there)
        def _():
            pl.semaphore_signal(
                barrier, inc=1, device_id=chip(me + offset), device_id_type=pl.DeviceIdType.MESH
            )

    pl.semaphore_wait(barrier, 3 + up.astype(jnp.int32) + down.astype(jnp.int32))

    for c in range(CHUNKS):
        own_copy(LOW, c).start()
        own_copy(HIGH, c).start()
    for t in range(per_half):
        pair_copy(t).start()
    for t in range(per_half):
        whole[core * per_half + t] = coeffs[:, t * tile : (t + 1) * tile]

    for r in range(3):

        @pl.when(jnp.logical_not(has_in[r]))
        def _():
            cross[r] = jnp.zeros_like(cross[r])

    sources = [me, *mates] + [mates[r] - GROUP * steps[r] for r in range(3)]
    for slot, source in enumerate(sources):
        at = pl.ds(slot * tile, tile)
        tiles[:tile, at] = picked_tile(me, alpha_list, alpha_kind, alpha_table, source).astype(BF16)
        tiles[tile:, at] = picked_tile(me, opp_list, opp_kind, opp_alpha_table, source).astype(BF16)

    def product(first, count, blocks):
        return jnp.dot(
            tiles[:, first * tile : (first + count) * tile],
            jnp.concatenate(blocks, axis=0),
            preferred_element_type=F32,
        )

    def beta_apply(data, kinds, table, j):
        left, right = [], []
        for link in range(beta_list.shape[1]):
            source = beta_list[j, link]
            left.append(data[source])
            right.append(table[kinds[j, link]])
        return lax.dot_general(
            jnp.concatenate(left, axis=1),
            jnp.concatenate(right, axis=1),
            (((1,), (1,)), ((), ())),
            preferred_element_type=F32,
        )

    def tile_at(j):
        return pl.ds(pl.multiple_of(j * tile, tile), tile)

    def z_start(r, c):
        there = has_out[r] & middle if r == DIAG else has_out[r]

        @pl.when(there)
        def _():
            z_copy(r, c).start()

    for c in range(CHUNKS):
        own_copy(LOW, c).wait_recv()
        z_start(LOW, c)
        if c % 2 == 0:
            relay_copy(c).start()
        own_copy(HIGH, c).wait_recv()
        z_start(HIGH, c)
        if c % 2 == 1:
            relay_copy(c).start()
        acc[:, columns(c)] = product(0, 3, [coeffs[:, columns(c)], plane[LOW, c], plane[HIGH, c]])

    for t in range(per_half):
        pair_copy(t).wait_recv()

    def cross_wait(r, c):
        @pl.when(has_in[r])
        def _():
            z_copy(r, c).wait_recv()

    def hop_start(src, c):
        @pl.when(has_in[src] & middle & (x == c % 2))
        def _():
            hop_copy(src, c).start()

    for c in range(CHUNKS):
        relay_copy(c).wait_recv()
        z_start(DIAG, c)
        cross_wait(LOW, c)
        hop_start(LOW, c)
        cross_wait(HIGH, c)
        hop_start(HIGH, c)

        @pl.loop(c * per_chunk, (c + 1) * per_chunk)
        def _(j):
            acc[:tile, tile_at(j)] += beta_apply(whole, beta_kind, beta_table, j)

    for c in range(CHUNKS):
        cross_wait(DIAG, c)
        total = acc[:, columns(c)] + product(3, 4, [plane[DIAG, c], cross[LOW, c], cross[HIGH, c], cross[DIAG, c]])
        for t in range(per_chunk):
            part = total[tile:, t * tile : (t + 1) * tile].astype(BF16)
            half[core * per_half + c * per_chunk + t] = part
        acc[:tile, columns(c)] = total[:tile]
        half_copy(c).start()

    for c in range(CHUNKS):
        half_copy(c).wait()

    @pl.loop(0, per_half)
    def _(j):
        out[:, tile_at(j)] = (acc[:tile, tile_at(j)] + beta_apply(half, opp_beta_kind, opp_beta_table, j)).astype(BF16)

    for t in range(per_half):
        pair_copy(t).wait_send()
    for c in range(CHUNKS):
        own_copy(LOW, c).wait_send()
        own_copy(HIGH, c).wait_send()
        relay_copy(c).wait_send()
        for r in range(3):

            @pl.when(has_out[r] & middle if r == DIAG else has_out[r])
            def _():
                z_copy(r, c).wait_send()

        for src in (LOW, HIGH):

            @pl.when(has_in[src] & middle & (x == c % 2))
            def _():
                hop_copy(src, c).wait_send()


def local(group_count, coeffs, *rest):
    lists, tables = rest[:7], rest[7:]
    flat = coeffs.reshape(coeffs.shape[1:])
    rows, cols = flat.shape
    width = cols // CHUNKS
    tile = tables[0].shape[1]
    vmem = pl.BlockSpec(memory_space=pltpu.VMEM)
    smem = pl.BlockSpec(memory_space=pltpu.SMEM)
    dma = pltpu.SemaphoreType.DMA
    sigma = pl.pallas_call(
        functools.partial(kernel, group_count),
        out_shape=jax.ShapeDtypeStruct((rows, cols), BF16),
        in_specs=[smem] * 7 + [vmem] * 5,
        out_specs=vmem,
        scratch_shapes=[
            pltpu.VMEM((3, CHUNKS, rows, width), BF16),
            pltpu.VMEM((3, CHUNKS, rows, width), BF16),
            pltpu.VMEM((2 * cols // tile, rows, tile), BF16),
            pltpu.VMEM((2 * cols // tile, rows, tile), BF16),
            pltpu.VMEM((2 * tile, cols), F32),
            pltpu.VMEM((2 * tile, 7 * tile), BF16),
            dma((2, CHUNKS)),
            dma((3, CHUNKS)),
            dma((CHUNKS,)),
            dma((3, CHUNKS)),
            dma((3, CHUNKS)),
            dma((2, CHUNKS)),
            dma((2, cols // tile)),
            dma((CHUNKS,)),
            dma((CHUNKS,)),
        ],
        compiler_params=pltpu.CompilerParams(
            collective_id=0, has_side_effects=True, vmem_limit_bytes=40 * 1024 * 1024
        ),
    )(*lists, flat, *tables)
    return sigma.reshape(coeffs.shape)


def solution(mesh):
    halves = P("beta", None)
    return jax.shard_map(
        functools.partial(local, mesh.shape["alpha"] // GROUP),
        mesh=mesh,
        in_specs=(P(None, "alpha", "beta"), halves, halves, halves) + (P(),) * 8,
        out_specs=P(None, "alpha", "beta"),
        check_vma=False,
    )
```

```python
import functools

import jax
import jax.numpy as jnp
from jax import lax
from jax.experimental import pallas as pl
from jax.experimental.pallas import tpu as pltpu
from jax.sharding import PartitionSpec as P

CHUNKS = 8
GROUP = 4
BF16, F32 = jnp.bfloat16, jnp.float32
LOW, HIGH, DIAG = range(3)


def picked_tile(block, lists, kinds, table, source):
    kind, found = jnp.int32(0), jnp.int32(0)
    for link in range(lists.shape[0]):
        hit = (lists[link, block] == source).astype(jnp.int32)
        kind += hit * kinds[link, block]
        found += hit
    return table[kind].astype(F32) * found.astype(F32)


def kernel(
    group_count,
    beta_list_hbm,
    beta_kind_hbm,
    opp_beta_kind_hbm,
    alpha_list_hbm,
    alpha_kind_hbm,
    opp_list_hbm,
    opp_kind_hbm,
    coeffs_hbm,
    beta_table_hbm,
    alpha_table_hbm,
    opp_alpha_table_hbm,
    opp_beta_table_hbm,
    out,
    beta_list,
    beta_kind,
    opp_beta_kind,
    alpha_list,
    alpha_kind,
    opp_list,
    opp_kind,
    coeffs,
    beta_table,
    alpha_table,
    opp_alpha_table,
    opp_beta_table,
    load_sem,
    plane,
    cross,
    whole,
    half,
    acc,
    tiles,
    own_send,
    plane_recv,
    relay_send,
    z_send,
    cross_recv,
    hop_send,
    pair_sem,
    half_send,
    half_recv,
):
    rows, cols = coeffs.shape
    width = cols // CHUNKS
    tile = beta_table.shape[1]
    per_half = cols // tile
    per_chunk = width // tile
    me, core = lax.axis_index("alpha"), lax.axis_index("beta")
    z, p = me // GROUP, me % GROUP
    x, y = p % 2, p // 2
    places = (p + 1 - 2 * x, p + 2 - 4 * y, 3 - p)
    mates = tuple(z * GROUP + q for q in places)
    steps = (1 - 2 * x, 1 - 2 * y, 1 - 2 * y)
    middle = x + y == 1

    def inside(group):
        return (group >= 0) & (group < group_count)

    has_out = [inside(z + step) for step in steps]
    has_in = [inside(z - step) for step in steps]

    def chip(index):
        return (index, core)

    pair = (me, 1 - core)

    def send(src, dst, send_sem, recv_sem, device):
        return pltpu.make_async_remote_copy(
            src_ref=src,
            dst_ref=dst,
            send_sem=send_sem,
            recv_sem=recv_sem,
            device_id=device,
            device_id_type=pl.DeviceIdType.MESH,
        )

    def columns(c):
        return pl.ds(c * width, width)

    def own_copy(to, c):
        return send(
            coeffs_hbm.at[:, columns(c)], plane.at[to, c], own_send.at[to, c], plane_recv.at[to, c], chip(mates[to])
        )

    def relay_copy(c):
        src, to = (LOW, HIGH) if c % 2 == 0 else (HIGH, LOW)
        return send(plane.at[src, c], plane.at[DIAG, c], relay_send.at[c], plane_recv.at[DIAG, c], chip(mates[to]))

    def z_copy(r, c):
        return send(
            plane.at[r, c], cross.at[r, c], z_send.at[r, c], cross_recv.at[r, c], chip(me + GROUP * steps[r])
        )

    def hop_copy(src, c):
        to = HIGH if src == LOW else LOW
        return send(cross.at[src, c], cross.at[DIAG, c], hop_send.at[src, c], cross_recv.at[DIAG, c], chip(mates[to]))

    def half_copy(c):
        part = half.at[pl.ds(core * per_half + c * per_chunk, per_chunk)]
        return send(part, part, half_send.at[c], half_recv.at[c], pair)

    def pair_copy(t):
        part = coeffs_hbm.at[:, pl.ds(t * tile, tile)]
        return send(part, whole.at[core * per_half + t], pair_sem.at[0, t], pair_sem.at[1, t], pair)

    loads = [
        pltpu.make_async_copy(src, dst, load_sem.at[k])
        for k, (src, dst) in enumerate(
            (
                (coeffs_hbm, coeffs),
                (alpha_list_hbm, alpha_list),
                (alpha_kind_hbm, alpha_kind),
                (opp_list_hbm, opp_list),
                (opp_kind_hbm, opp_kind),
                (alpha_table_hbm, alpha_table),
                (opp_alpha_table_hbm, opp_alpha_table),
                (beta_list_hbm, beta_list),
                (beta_kind_hbm, beta_kind),
                (opp_beta_kind_hbm, opp_beta_kind),
                (beta_table_hbm, beta_table),
                (opp_beta_table_hbm, opp_beta_table),
            )
        )
    ]
    for load in loads:
        load.start()

    barrier = pltpu.get_barrier_semaphore()
    for device in (chip(mates[LOW]), chip(mates[HIGH]), pair):
        pl.semaphore_signal(barrier, inc=1, device_id=device, device_id_type=pl.DeviceIdType.MESH)
    up, down = inside(z + 1), inside(z - 1)
    for there, offset in ((up, GROUP), (down, -GROUP)):

        @pl.when(there)
        def _():
            pl.semaphore_signal(
                barrier, inc=1, device_id=chip(me + offset), device_id_type=pl.DeviceIdType.MESH
            )

    pl.semaphore_wait(barrier, 3 + up.astype(jnp.int32) + down.astype(jnp.int32))

    for c in range(CHUNKS):
        own_copy(LOW, c).start()
        own_copy(HIGH, c).start()
    for t in range(per_half):
        pair_copy(t).start()
    for load in loads:
        load.wait()
    for t in range(per_half):
        whole[core * per_half + t] = coeffs[:, t * tile : (t + 1) * tile]

    for r in range(3):

        @pl.when(jnp.logical_not(has_in[r]))
        def _():
            cross[r] = jnp.zeros_like(cross[r])

    sources = [me, *mates] + [mates[r] - GROUP * steps[r] for r in range(3)]
    for slot, source in enumerate(sources):
        at = pl.ds(slot * tile, tile)
        tiles[:tile, at] = picked_tile(me, alpha_list, alpha_kind, alpha_table, source).astype(BF16)
        tiles[tile:, at] = picked_tile(me, opp_list, opp_kind, opp_alpha_table, source).astype(BF16)

    def product(first, count, blocks):
        return jnp.dot(
            tiles[:, first * tile : (first + count) * tile],
            jnp.concatenate(blocks, axis=0),
            preferred_element_type=F32,
        )

    def beta_apply(data, kinds, table, j):
        left, right = [], []
        for link in range(beta_list.shape[0]):
            source = beta_list[link, j]
            left.append(data[source])
            right.append(table[kinds[link, j]])
        return lax.dot_general(
            jnp.concatenate(left, axis=1),
            jnp.concatenate(right, axis=1),
            (((1,), (1,)), ((), ())),
            preferred_element_type=F32,
        )

    def tile_at(j):
        return pl.ds(pl.multiple_of(j * tile, tile), tile)

    def z_start(r, c):
        there = has_out[r] & middle if r == DIAG else has_out[r]

        @pl.when(there)
        def _():
            z_copy(r, c).start()

    for c in range(CHUNKS):
        own_copy(LOW, c).wait_recv()
        z_start(LOW, c)
        if c % 2 == 0:
            relay_copy(c).start()
        own_copy(HIGH, c).wait_recv()
        z_start(HIGH, c)
        if c % 2 == 1:
            relay_copy(c).start()
        acc[:, columns(c)] = product(0, 3, [coeffs[:, columns(c)], plane[LOW, c], plane[HIGH, c]])

    for t in range(per_half):
        pair_copy(t).wait_recv()

    def cross_wait(r, c):
        @pl.when(has_in[r])
        def _():
            z_copy(r, c).wait_recv()

    def hop_start(src, c):
        @pl.when(has_in[src] & middle & (x == c % 2))
        def _():
            hop_copy(src, c).start()

    for c in range(CHUNKS):
        relay_copy(c).wait_recv()
        z_start(DIAG, c)
        cross_wait(LOW, c)
        hop_start(LOW, c)
        cross_wait(HIGH, c)
        hop_start(HIGH, c)

        @pl.loop(c * per_chunk, (c + 1) * per_chunk)
        def _(j):
            acc[:tile, tile_at(j)] += beta_apply(whole, beta_kind, beta_table, j)

    for c in range(CHUNKS):
        cross_wait(DIAG, c)
        total = acc[:, columns(c)] + product(3, 4, [plane[DIAG, c], cross[LOW, c], cross[HIGH, c], cross[DIAG, c]])
        for t in range(per_chunk):
            part = total[tile:, t * tile : (t + 1) * tile].astype(BF16)
            half[core * per_half + c * per_chunk + t] = part
        acc[:tile, columns(c)] = total[:tile]
        half_copy(c).start()

    for c in range(CHUNKS):
        half_copy(c).wait()

    @pl.loop(0, per_half)
    def _(j):
        out[:, tile_at(j)] = (acc[:tile, tile_at(j)] + beta_apply(half, opp_beta_kind, opp_beta_table, j)).astype(BF16)

    for t in range(per_half):
        pair_copy(t).wait_send()
    for c in range(CHUNKS):
        own_copy(LOW, c).wait_send()
        own_copy(HIGH, c).wait_send()
        relay_copy(c).wait_send()
        for r in range(3):

            @pl.when(has_out[r] & middle if r == DIAG else has_out[r])
            def _():
                z_copy(r, c).wait_send()

        for src in (LOW, HIGH):

            @pl.when(has_in[src] & middle & (x == c % 2))
            def _():
                hop_copy(src, c).wait_send()


def local(group_count, coeffs, *rest):
    lists, tables = rest[:7], rest[7:]
    flat = coeffs.reshape(coeffs.shape[1:])
    rows, cols = flat.shape
    width = cols // CHUNKS
    tile = tables[0].shape[1]
    vmem = pl.BlockSpec(memory_space=pltpu.VMEM)
    hbm = pl.BlockSpec(memory_space=pltpu.HBM)
    operands = (*(one.T for one in lists), flat, *tables)
    in_lists = [pltpu.SMEM(one.shape, one.dtype) for one in operands[:7]]
    in_arrays = [pltpu.VMEM(one.shape, one.dtype) for one in operands[7:]]
    dma = pltpu.SemaphoreType.DMA
    sigma = pl.pallas_call(
        functools.partial(kernel, group_count),
        out_shape=jax.ShapeDtypeStruct((rows, cols), BF16),
        in_specs=[hbm] * len(operands),
        out_specs=vmem,
        scratch_shapes=[
            *in_lists,
            *in_arrays,
            dma((len(operands),)),
            pltpu.VMEM((3, CHUNKS, rows, width), BF16),
            pltpu.VMEM((3, CHUNKS, rows, width), BF16),
            pltpu.VMEM((2 * cols // tile, rows, tile), BF16),
            pltpu.VMEM((2 * cols // tile, rows, tile), BF16),
            pltpu.VMEM((2 * tile, cols), F32),
            pltpu.VMEM((2 * tile, 7 * tile), BF16),
            dma((2, CHUNKS)),
            dma((3, CHUNKS)),
            dma((CHUNKS,)),
            dma((3, CHUNKS)),
            dma((3, CHUNKS)),
            dma((2, CHUNKS)),
            dma((2, cols // tile)),
            dma((CHUNKS,)),
            dma((CHUNKS,)),
        ],
        compiler_params=pltpu.CompilerParams(
            collective_id=0, has_side_effects=True, vmem_limit_bytes=60 * 1024 * 1024
        ),
    )(*operands)
    return sigma.reshape(coeffs.shape)


def solution(mesh):
    halves = P("beta", None)
    return jax.shard_map(
        functools.partial(local, mesh.shape["alpha"] // GROUP),
        mesh=mesh,
        in_specs=(P(None, "alpha", "beta"), halves, halves, halves) + (P(),) * 8,
        out_specs=P(None, "alpha", "beta"),
        check_vma=False,
    )
```

```python
import functools

import jax
import jax.numpy as jnp
from jax import lax
from jax.experimental import pallas as pl
from jax.experimental.pallas import tpu as pltpu
from jax.sharding import PartitionSpec as P

CHUNKS = 8
GROUP = 4
UNROLL = 4
BF16, F32 = jnp.bfloat16, jnp.float32
LOW, HIGH, DIAG = range(3)


def picked_tile(block, lists, kinds, table, source):
    kind, found = jnp.int32(0), jnp.int32(0)
    for link in range(lists.shape[0]):
        hit = (lists[link, block] == source).astype(jnp.int32)
        kind += hit * kinds[link, block]
        found += hit
    return table[kind].astype(F32) * found.astype(F32)


def kernel(
    group_count,
    beta_list_hbm,
    beta_kind_hbm,
    opp_beta_kind_hbm,
    alpha_list_hbm,
    alpha_kind_hbm,
    opp_list_hbm,
    opp_kind_hbm,
    coeffs_hbm,
    beta_table_hbm,
    alpha_table_hbm,
    opp_alpha_table_hbm,
    opp_beta_table_hbm,
    out,
    beta_list,
    beta_kind,
    opp_beta_kind,
    alpha_list,
    alpha_kind,
    opp_list,
    opp_kind,
    coeffs,
    beta_table,
    alpha_table,
    opp_alpha_table,
    opp_beta_table,
    load_sem,
    plane,
    cross,
    whole,
    half,
    acc,
    mine,
    tiles,
    own_send,
    plane_recv,
    relay_send,
    z_send,
    cross_recv,
    hop_send,
    pair_sem,
    half_send,
    half_recv,
):
    rows, cols = coeffs.shape
    width = cols // CHUNKS
    tile = beta_table.shape[1]
    per_half = cols // tile
    per_chunk = width // tile
    me, core = lax.axis_index("alpha"), lax.axis_index("beta")
    z, p = me // GROUP, me % GROUP
    x, y = p % 2, p // 2
    places = (p + 1 - 2 * x, p + 2 - 4 * y, 3 - p)
    mates = tuple(z * GROUP + q for q in places)
    steps = (1 - 2 * x, 1 - 2 * y, 1 - 2 * y)
    middle = x + y == 1

    def inside(group):
        return (group >= 0) & (group < group_count)

    has_out = [inside(z + step) for step in steps]
    has_in = [inside(z - step) for step in steps]

    def chip(index):
        return (index, core)

    pair = (me, 1 - core)

    def send(src, dst, send_sem, recv_sem, device):
        return pltpu.make_async_remote_copy(
            src_ref=src,
            dst_ref=dst,
            send_sem=send_sem,
            recv_sem=recv_sem,
            device_id=device,
            device_id_type=pl.DeviceIdType.MESH,
        )

    def columns(c):
        return pl.ds(c * width, width)

    def own_copy(to, c):
        return send(
            coeffs_hbm.at[:, columns(c)], plane.at[to, c], own_send.at[to, c], plane_recv.at[to, c], chip(mates[to])
        )

    def relay_copy(c):
        src, to = (LOW, HIGH) if c % 2 == 0 else (HIGH, LOW)
        return send(plane.at[src, c], plane.at[DIAG, c], relay_send.at[c], plane_recv.at[DIAG, c], chip(mates[to]))

    def z_copy(r, c):
        return send(
            plane.at[r, c], cross.at[r, c], z_send.at[r, c], cross_recv.at[r, c], chip(me + GROUP * steps[r])
        )

    def hop_copy(src, c):
        to = HIGH if src == LOW else LOW
        return send(cross.at[src, c], cross.at[DIAG, c], hop_send.at[src, c], cross_recv.at[DIAG, c], chip(mates[to]))

    def half_copy(c):
        part = half.at[pl.ds(core * per_half + c * per_chunk, per_chunk)]
        return send(part, part, half_send.at[c], half_recv.at[c], pair)

    def pair_copy(t):
        part = coeffs_hbm.at[:, pl.ds(t * tile, tile)]
        return send(part, whole.at[core * per_half + t], pair_sem.at[0, t], pair_sem.at[1, t], pair)

    loads = [
        pltpu.make_async_copy(src, dst, load_sem.at[k])
        for k, (src, dst) in enumerate(
            (
                (coeffs_hbm, coeffs),
                (alpha_list_hbm, alpha_list),
                (alpha_kind_hbm, alpha_kind),
                (opp_list_hbm, opp_list),
                (opp_kind_hbm, opp_kind),
                (alpha_table_hbm, alpha_table),
                (opp_alpha_table_hbm, opp_alpha_table),
                (beta_list_hbm, beta_list),
                (beta_kind_hbm, beta_kind),
                (opp_beta_kind_hbm, opp_beta_kind),
                (beta_table_hbm, beta_table),
                (opp_beta_table_hbm, opp_beta_table),
            )
        )
    ]
    for load in loads:
        load.start()

    barrier = pltpu.get_barrier_semaphore()
    for device in (chip(mates[LOW]), chip(mates[HIGH]), pair):
        pl.semaphore_signal(barrier, inc=1, device_id=device, device_id_type=pl.DeviceIdType.MESH)
    up, down = inside(z + 1), inside(z - 1)
    for there, offset in ((up, GROUP), (down, -GROUP)):

        @pl.when(there)
        def _():
            pl.semaphore_signal(
                barrier, inc=1, device_id=chip(me + offset), device_id_type=pl.DeviceIdType.MESH
            )

    pl.semaphore_wait(barrier, 3 + up.astype(jnp.int32) + down.astype(jnp.int32))

    for c in range(CHUNKS):
        own_copy(LOW, c).start()
        own_copy(HIGH, c).start()
    for t in range(per_half):
        pair_copy(t).start()
    for load in loads:
        load.wait()
    for t in range(per_half):
        whole[core * per_half + t] = coeffs[:, t * tile : (t + 1) * tile]

    for r in range(3):

        @pl.when(jnp.logical_not(has_in[r]))
        def _():
            cross[r] = jnp.zeros_like(cross[r])

    sources = [me, *mates] + [mates[r] - GROUP * steps[r] for r in range(3)]
    for slot, source in enumerate(sources):
        at = pl.ds(slot * tile, tile)
        tiles[:tile, at] = picked_tile(me, alpha_list, alpha_kind, alpha_table, source).astype(BF16)
        tiles[tile:, at] = picked_tile(me, opp_list, opp_kind, opp_alpha_table, source).astype(BF16)

    def product(first, count, blocks):
        return jnp.dot(
            tiles[:, first * tile : (first + count) * tile],
            jnp.concatenate(blocks, axis=0),
            preferred_element_type=F32,
        )

    def beta_apply(data, kinds, table, j):
        left, right = [], []
        for link in range(beta_list.shape[0]):
            source = beta_list[link, j]
            left.append(data[source])
            right.append(table[kinds[link, j]])
        return lax.dot_general(
            jnp.concatenate(left, axis=1),
            jnp.concatenate(right, axis=1),
            (((1,), (1,)), ((), ())),
            preferred_element_type=F32,
        )

    def tile_at(j):
        return pl.ds(pl.multiple_of(j * tile, tile), tile)

    def z_start(r, c):
        there = has_out[r] & middle if r == DIAG else has_out[r]

        @pl.when(there)
        def _():
            z_copy(r, c).start()

    def beta_add(step):
        span = 2 * per_chunk

        @pl.loop(step * span, (step + 1) * span, unroll=UNROLL)
        def _(j):
            mine[:, tile_at(j)] = beta_apply(whole, beta_kind, beta_table, j)

    for c in range(CHUNKS):
        own_copy(LOW, c).wait_recv()
        z_start(LOW, c)
        if c % 2 == 0:
            relay_copy(c).start()
        own_copy(HIGH, c).wait_recv()
        z_start(HIGH, c)
        if c % 2 == 1:
            relay_copy(c).start()
        acc[:, columns(c)] = product(0, 3, [coeffs[:, columns(c)], plane[LOW, c], plane[HIGH, c]])
        if c == CHUNKS // 2 - 1:
            for t in range(per_half):
                pair_copy(t).wait_recv()
        if c >= CHUNKS // 2:
            beta_add(c - CHUNKS // 2)

    def cross_wait(r, c, there):
        @pl.when(has_in[r] & there)
        def _():
            z_copy(r, c).wait_recv()

    def hop_start(src, c):
        @pl.when(has_in[src] & middle & (x == c % 2))
        def _():
            hop_copy(src, c).start()

    for c in range(CHUNKS):
        relay_copy(c).wait_recv()
        z_start(DIAG, c)
        for r in (LOW, HIGH):
            cross_wait(r, c, middle)
            hop_start(r, c)

    for c in range(CHUNKS):
        cross_wait(LOW, c, jnp.logical_not(middle))
        cross_wait(HIGH, c, jnp.logical_not(middle))
        cross_wait(DIAG, c, True)
        total = acc[:, columns(c)] + product(3, 4, [plane[DIAG, c], cross[LOW, c], cross[HIGH, c], cross[DIAG, c]])
        for t in range(per_chunk):
            part = total[tile:, t * tile : (t + 1) * tile].astype(BF16)
            half[core * per_half + c * per_chunk + t] = part
        mine[:, columns(c)] += total[:tile]
        half_copy(c).start()

    for c in range(CHUNKS):
        half_copy(c).wait()

    @pl.loop(0, per_half, unroll=UNROLL)
    def _(j):
        mixed = beta_apply(half, opp_beta_kind, opp_beta_table, j)
        out[:, tile_at(j)] = (mine[:, tile_at(j)] + mixed).astype(BF16)

    for t in range(per_half):
        pair_copy(t).wait_send()
    for c in range(CHUNKS):
        own_copy(LOW, c).wait_send()
        own_copy(HIGH, c).wait_send()
        relay_copy(c).wait_send()
        for r in range(3):

            @pl.when(has_out[r] & middle if r == DIAG else has_out[r])
            def _():
                z_copy(r, c).wait_send()

        for src in (LOW, HIGH):

            @pl.when(has_in[src] & middle & (x == c % 2))
            def _():
                hop_copy(src, c).wait_send()


def local(group_count, coeffs, *rest):
    lists, tables = rest[:7], rest[7:]
    flat = coeffs.reshape(coeffs.shape[1:])
    rows, cols = flat.shape
    width = cols // CHUNKS
    tile = tables[0].shape[1]
    vmem = pl.BlockSpec(memory_space=pltpu.VMEM)
    hbm = pl.BlockSpec(memory_space=pltpu.HBM)
    operands = (*(one.T for one in lists), flat, *tables)
    in_lists = [pltpu.SMEM(one.shape, one.dtype) for one in operands[:7]]
    in_arrays = [pltpu.VMEM(one.shape, one.dtype) for one in operands[7:]]
    dma = pltpu.SemaphoreType.DMA
    sigma = pl.pallas_call(
        functools.partial(kernel, group_count),
        out_shape=jax.ShapeDtypeStruct((rows, cols), BF16),
        in_specs=[hbm] * len(operands),
        out_specs=vmem,
        scratch_shapes=[
            *in_lists,
            *in_arrays,
            dma((len(operands),)),
            pltpu.VMEM((3, CHUNKS, rows, width), BF16),
            pltpu.VMEM((3, CHUNKS, rows, width), BF16),
            pltpu.VMEM((2 * cols // tile, rows, tile), BF16),
            pltpu.VMEM((2 * cols // tile, rows, tile), BF16),
            pltpu.VMEM((2 * tile, cols), F32),
            pltpu.VMEM((rows, cols), F32),
            pltpu.VMEM((2 * tile, 7 * tile), BF16),
            dma((2, CHUNKS)),
            dma((3, CHUNKS)),
            dma((CHUNKS,)),
            dma((3, CHUNKS)),
            dma((3, CHUNKS)),
            dma((2, CHUNKS)),
            dma((2, cols // tile)),
            dma((CHUNKS,)),
            dma((CHUNKS,)),
        ],
        compiler_params=pltpu.CompilerParams(
            collective_id=0, has_side_effects=True, vmem_limit_bytes=60 * 1024 * 1024
        ),
    )(*operands)
    return sigma.reshape(coeffs.shape)


def solution(mesh):
    halves = P("beta", None)
    return jax.shard_map(
        functools.partial(local, mesh.shape["alpha"] // GROUP),
        mesh=mesh,
        in_specs=(P(None, "alpha", "beta"), halves, halves, halves) + (P(),) * 8,
        out_specs=P(None, "alpha", "beta"),
        check_vma=False,
    )
```

```python
import functools

import jax
import jax.numpy as jnp
from jax import lax
from jax.experimental import pallas as pl
from jax.experimental.pallas import tpu as pltpu
from jax.sharding import PartitionSpec as P

CHUNKS = 8
GROUP = 4
UNROLL = 4
BF16, F32 = jnp.bfloat16, jnp.float32
LOW, HIGH, DIAG = range(3)


def picked_tile(block, lists, kinds, table, source):
    kind, found = jnp.int32(0), jnp.int32(0)
    for link in range(lists.shape[0]):
        hit = (lists[link, block] == source).astype(jnp.int32)
        kind += hit * kinds[link, block]
        found += hit
    return table[kind].astype(F32) * found.astype(F32)


def kernel(
    group_count,
    beta_list_hbm,
    beta_kind_hbm,
    opp_beta_kind_hbm,
    alpha_list_hbm,
    alpha_kind_hbm,
    opp_list_hbm,
    opp_kind_hbm,
    coeffs_hbm,
    beta_table_hbm,
    alpha_table_hbm,
    opp_alpha_table_hbm,
    opp_beta_table_hbm,
    out,
    beta_list,
    beta_kind,
    opp_beta_kind,
    alpha_list,
    alpha_kind,
    opp_list,
    opp_kind,
    coeffs,
    beta_table,
    alpha_table,
    opp_alpha_table,
    opp_beta_table,
    load_sem,
    plane,
    cross,
    whole,
    half,
    acc,
    mine,
    sigma,
    out_sem,
    tiles,
    own_send,
    plane_recv,
    relay_send,
    z_send,
    cross_recv,
    hop_send,
    pair_sem,
    half_send,
    half_recv,
):
    rows, cols = coeffs.shape
    width = cols // CHUNKS
    tile = beta_table.shape[1]
    per_half = cols // tile
    per_chunk = width // tile
    me, core = lax.axis_index("alpha"), lax.axis_index("beta")
    z, p = me // GROUP, me % GROUP
    x, y = p % 2, p // 2
    places = (p + 1 - 2 * x, p + 2 - 4 * y, 3 - p)
    mates = tuple(z * GROUP + q for q in places)
    steps = (1 - 2 * x, 1 - 2 * y, 1 - 2 * y)
    middle = x + y == 1

    def inside(group):
        return (group >= 0) & (group < group_count)

    has_out = [inside(z + step) for step in steps]
    has_in = [inside(z - step) for step in steps]

    def chip(index):
        return (index, core)

    pair = (me, 1 - core)

    def send(src, dst, send_sem, recv_sem, device):
        return pltpu.make_async_remote_copy(
            src_ref=src,
            dst_ref=dst,
            send_sem=send_sem,
            recv_sem=recv_sem,
            device_id=device,
            device_id_type=pl.DeviceIdType.MESH,
        )

    def columns(c):
        return pl.ds(c * width, width)

    def own_copy(to, c):
        return send(
            coeffs.at[:, columns(c)], plane.at[to, c], own_send.at[to, c], plane_recv.at[to, c], chip(mates[to])
        )

    def relay_copy(c):
        src, to = (LOW, HIGH) if c % 2 == 0 else (HIGH, LOW)
        return send(plane.at[src, c], plane.at[DIAG, c], relay_send.at[c], plane_recv.at[DIAG, c], chip(mates[to]))

    def z_copy(r, c):
        return send(
            plane.at[r, c], cross.at[r, c], z_send.at[r, c], cross_recv.at[r, c], chip(me + GROUP * steps[r])
        )

    def hop_copy(src, c):
        to = HIGH if src == LOW else LOW
        return send(cross.at[src, c], cross.at[DIAG, c], hop_send.at[src, c], cross_recv.at[DIAG, c], chip(mates[to]))

    def half_copy(c):
        part = half.at[pl.ds(core * per_half + c * per_chunk, per_chunk)]
        return send(part, part, half_send.at[c], half_recv.at[c], pair)

    def pair_copy(t):
        part = coeffs_hbm.at[:, pl.ds(t * tile, tile)]
        return send(part, whole.at[core * per_half + t], pair_sem.at[0, t], pair_sem.at[1, t], pair)

    loads = [
        pltpu.make_async_copy(src, dst, load_sem.at[k])
        for k, (src, dst) in enumerate(
            (
                (coeffs_hbm, coeffs),
                (alpha_list_hbm, alpha_list),
                (alpha_kind_hbm, alpha_kind),
                (opp_list_hbm, opp_list),
                (opp_kind_hbm, opp_kind),
                (alpha_table_hbm, alpha_table),
                (opp_alpha_table_hbm, opp_alpha_table),
                (beta_list_hbm, beta_list),
                (beta_kind_hbm, beta_kind),
                (opp_beta_kind_hbm, opp_beta_kind),
                (beta_table_hbm, beta_table),
                (opp_beta_table_hbm, opp_beta_table),
            )
        )
    ]
    for load in loads:
        load.start()

    barrier = pltpu.get_barrier_semaphore()
    for device in (chip(mates[LOW]), chip(mates[HIGH]), pair):
        pl.semaphore_signal(barrier, inc=1, device_id=device, device_id_type=pl.DeviceIdType.MESH)
    up, down = inside(z + 1), inside(z - 1)
    for there, offset in ((up, GROUP), (down, -GROUP)):

        @pl.when(there)
        def _():
            pl.semaphore_signal(
                barrier, inc=1, device_id=chip(me + offset), device_id_type=pl.DeviceIdType.MESH
            )

    pl.semaphore_wait(barrier, 3 + up.astype(jnp.int32) + down.astype(jnp.int32))

    loads[0].wait()
    for c in range(CHUNKS):
        own_copy(LOW, c).start()
        own_copy(HIGH, c).start()
    for t in range(per_half):
        pair_copy(t).start()
    for load in loads[1:]:
        load.wait()
    for t in range(per_half):
        whole[core * per_half + t] = coeffs[:, t * tile : (t + 1) * tile]

    for r in range(3):

        @pl.when(jnp.logical_not(has_in[r]))
        def _():
            cross[r] = jnp.zeros_like(cross[r])

    sources = [me, *mates] + [mates[r] - GROUP * steps[r] for r in range(3)]
    for slot, source in enumerate(sources):
        at = pl.ds(slot * tile, tile)
        tiles[:tile, at] = picked_tile(me, alpha_list, alpha_kind, alpha_table, source).astype(BF16)
        tiles[tile:, at] = picked_tile(me, opp_list, opp_kind, opp_alpha_table, source).astype(BF16)

    def product(first, count, blocks):
        return jnp.dot(
            tiles[:, first * tile : (first + count) * tile],
            jnp.concatenate(blocks, axis=0),
            preferred_element_type=F32,
        )

    def beta_apply(data, kinds, table, j):
        left, right = [], []
        for link in range(beta_list.shape[0]):
            source = beta_list[link, j]
            left.append(data[source])
            right.append(table[kinds[link, j]])
        return lax.dot_general(
            jnp.concatenate(left, axis=1),
            jnp.concatenate(right, axis=1),
            (((1,), (1,)), ((), ())),
            preferred_element_type=F32,
        )

    def tile_at(j):
        return pl.ds(pl.multiple_of(j * tile, tile), tile)

    def z_start(r, c):
        there = has_out[r] & middle if r == DIAG else has_out[r]

        @pl.when(there)
        def _():
            z_copy(r, c).start()

    def beta_add(step):
        span = 2 * per_chunk

        @pl.loop(step * span, (step + 1) * span, unroll=UNROLL)
        def _(j):
            mine[:, tile_at(j)] = beta_apply(whole, beta_kind, beta_table, j)

    for c in range(CHUNKS):
        own_copy(LOW, c).wait_recv()
        z_start(LOW, c)
        if c % 2 == 0:
            relay_copy(c).start()
        own_copy(HIGH, c).wait_recv()
        z_start(HIGH, c)
        if c % 2 == 1:
            relay_copy(c).start()
        acc[:, columns(c)] = product(0, 3, [coeffs[:, columns(c)], plane[LOW, c], plane[HIGH, c]])
        if c == CHUNKS // 2 - 1:
            for t in range(per_half):
                pair_copy(t).wait_recv()
        if c >= CHUNKS // 2:
            beta_add(c - CHUNKS // 2)

    def cross_wait(r, c, there):
        @pl.when(has_in[r] & there)
        def _():
            z_copy(r, c).wait_recv()

    def hop_start(src, c):
        @pl.when(has_in[src] & middle & (x == c % 2))
        def _():
            hop_copy(src, c).start()

    for c in range(CHUNKS):
        relay_copy(c).wait_recv()
        z_start(DIAG, c)
        for r in (LOW, HIGH):
            cross_wait(r, c, middle)
            hop_start(r, c)

    for c in range(CHUNKS):
        cross_wait(LOW, c, jnp.logical_not(middle))
        cross_wait(HIGH, c, jnp.logical_not(middle))
        cross_wait(DIAG, c, True)
        total = acc[:, columns(c)] + product(3, 4, [plane[DIAG, c], cross[LOW, c], cross[HIGH, c], cross[DIAG, c]])
        for t in range(per_chunk):
            part = total[tile:, t * tile : (t + 1) * tile].astype(BF16)
            half[core * per_half + c * per_chunk + t] = part
        mine[:, columns(c)] += total[:tile]
        half_copy(c).start()

    for c in range(CHUNKS):
        half_copy(c).wait()

    def out_copy(k):
        at = pl.ds(k * UNROLL * tile, UNROLL * tile)
        return pltpu.make_async_copy(sigma.at[:, at], out.at[:, at], out_sem.at[k])

    for j in range(per_half):
        at = pl.ds(j * tile, tile)
        mixed = beta_apply(half, opp_beta_kind, opp_beta_table, j)
        sigma[:, at] = (mine[:, at] + mixed).astype(BF16)
        if j % UNROLL == UNROLL - 1:
            out_copy(j // UNROLL).start()

    for k in range(per_half // UNROLL):
        out_copy(k).wait()
    for t in range(per_half):
        pair_copy(t).wait_send()
    for c in range(CHUNKS):
        own_copy(LOW, c).wait_send()
        own_copy(HIGH, c).wait_send()
        relay_copy(c).wait_send()
        for r in range(3):

            @pl.when(has_out[r] & middle if r == DIAG else has_out[r])
            def _():
                z_copy(r, c).wait_send()

        for src in (LOW, HIGH):

            @pl.when(has_in[src] & middle & (x == c % 2))
            def _():
                hop_copy(src, c).wait_send()


def local(group_count, coeffs, *rest):
    lists, tables = rest[:7], rest[7:]
    flat = coeffs.reshape(coeffs.shape[1:])
    rows, cols = flat.shape
    width = cols // CHUNKS
    tile = tables[0].shape[1]
    hbm = pl.BlockSpec(memory_space=pltpu.HBM)
    operands = (*(one.T for one in lists), flat, *tables)
    in_lists = [pltpu.SMEM(one.shape, one.dtype) for one in operands[:7]]
    in_arrays = [pltpu.VMEM(one.shape, one.dtype) for one in operands[7:]]
    dma = pltpu.SemaphoreType.DMA
    result = pl.pallas_call(
        functools.partial(kernel, group_count),
        out_shape=jax.ShapeDtypeStruct((rows, cols), BF16),
        in_specs=[hbm] * len(operands),
        out_specs=hbm,
        scratch_shapes=[
            *in_lists,
            *in_arrays,
            dma((len(operands),)),
            pltpu.VMEM((3, CHUNKS, rows, width), BF16),
            pltpu.VMEM((3, CHUNKS, rows, width), BF16),
            pltpu.VMEM((2 * cols // tile, rows, tile), BF16),
            pltpu.VMEM((2 * cols // tile, rows, tile), BF16),
            pltpu.VMEM((2 * tile, cols), F32),
            pltpu.VMEM((rows, cols), F32),
            pltpu.VMEM((rows, cols), BF16),
            dma((cols // tile // UNROLL,)),
            pltpu.VMEM((2 * tile, 7 * tile), BF16),
            dma((2, CHUNKS)),
            dma((3, CHUNKS)),
            dma((CHUNKS,)),
            dma((3, CHUNKS)),
            dma((3, CHUNKS)),
            dma((2, CHUNKS)),
            dma((2, cols // tile)),
            dma((CHUNKS,)),
            dma((CHUNKS,)),
        ],
        compiler_params=pltpu.CompilerParams(
            collective_id=0, has_side_effects=True, vmem_limit_bytes=60 * 1024 * 1024
        ),
    )(*operands)
    return result.reshape(coeffs.shape)


def solution(mesh):
    halves = P("beta", None)
    return jax.shard_map(
        functools.partial(local, mesh.shape["alpha"] // GROUP),
        mesh=mesh,
        in_specs=(P(None, "alpha", "beta"), halves, halves, halves) + (P(),) * 8,
        out_specs=P(None, "alpha", "beta"),
        check_vma=False,
    )
```
